1024 devices in a mesh: replica: 16 (over z_lo), fsdp: 8 (over y, z_hi), tensor: 8 (over x, core).
Axes of the slice: x: 4, y: 4, z: 32 (z_hi: 2, z_lo: 16; z = z_hi * 16 + z_lo), core: 2. Of those that a mesh axis runs over, the one named last changes fastest.
Arguments:
- activations: bfloat16 [16384, 8192], P(('replica', 'fsdp')), may hold values from -6 to 6
- value_grads: bfloat16 [16384, 2048], P(('replica', 'fsdp'), 'tensor'), may hold values from -6 to 6
- lengths: int32 [256], P(('replica', 'fsdp')), may hold values from 16 to 64, as said below
- master: float32 [8192, 2048], P('fsdp', 'tensor'), may hold values from -0.0625 to 0.0625
- moment_one: float32 [8192, 2048], P('fsdp', 'tensor'), may hold values from -0.078125 to 0.078125
- moment_two: float32 [8192, 2048], P('fsdp', 'tensor'), may hold values from 1e-06 to 0.0001
Outputs:
- input_grads: bfloat16 [16384, 8192], P(('replica', 'fsdp'), 'tensor')
- new_master: float32 [8192, 2048], P('fsdp', 'tensor')
- new_moment_one: float32 [8192, 2048], P('fsdp', 'tensor')
- new_moment_two: float32 [8192, 2048], P('fsdp', 'tensor')
The draws below stay inside these ranges and needn't reach their ends.
Inputs may be any that keep to these rules, and one draw needn't show every extreme that they name: `lengths`: each sequence's live tokens form a prefix of its 64 positions.
All inputs are finite; a program needn't handle non-finite values.
Results may differ from the reference program's by a relative error of at most 0.014.
Values may be sent and summed in bfloat16 or wider, within the bound.
No kernel may reach another device: no remote copies, remote signals or barrier semaphores. Data moves between devices by JAX's collectives and lax.ppermute only.
A program may use at most 64 MiB of HBM per device.

```python
import math
import jax
import jax.numpy as jnp
from jax import lax

D = 8192
SEQ = 64
KV = 2048
TOK_DEV = 128
SEQS = 256
TOKENS = 16384
N_REPLICA = 16
N_FSDP = 8
N_TENSOR = 8


def draw_lengths(key, part):
    values = jax.random.randint(key, (SEQS,), SEQ // 4, SEQ + 1, dtype=jnp.int32)
    return values.at[0].set(SEQ)


def shard_levels(own_key, extent, split, least, high):
    def one(dim, parts):
        steps = jax.random.uniform(jax.random.fold_in(jax.random.fold_in(own_key, 6), dim), (parts,), jnp.float32, least / len(split), high / len(split))
        return jnp.repeat(jnp.exp(steps), extent[dim] // parts).reshape((-1,) + (1,) * (len(extent) - dim - 1))

    level = one(*split[0])
    for cut in split[1:]:
        level = level * one(*cut)
    return level


def noise(rng, shape, spread, reach, split=(), held_as=jnp.bfloat16):
    gain = shard_levels(rng, shape, split, -0.22, 0.18) if split else 1.0
    result = jax.random.normal(rng, shape, jnp.float32) * spread * gain
    return jnp.minimum(jnp.maximum(result, -reach), reach).astype(held_as)


def setup_inputs(seed: int = 0) -> dict:
    key_list = jax.random.split(jax.random.key(seed), 7)
    activations = noise(key_list[0], (TOKENS, D), 1.0, 6.0, ((0, 128),))
    value_grads = noise(key_list[1], (TOKENS, KV), 1.0, 6.0, ((0, 128), (1, 8)))
    lengths = draw_lengths(jax.random.fold_in(key_list[6], 71), 0)
    master = noise(key_list[3], (D, KV), D ** -0.5, 0.0625, ((0, 8), (1, 8)), jnp.float32)
    moment_one = noise(key_list[4], (D, KV), 0.005, 0.078125, ((0, 8), (1, 8)), jnp.float32)
    moment_two = jnp.clip(jnp.exp(math.log(0.0001) - 4.6051702 * jax.random.uniform(key_list[5], (D, KV), jnp.float32) ** shard_levels(key_list[5], (D, KV), ((0, 8), (1, 8)), -0.2, 0.2)), 9.999999974752427e-07, 0.0001)
    return dict(activations=activations, value_grads=value_grads, lengths=lengths, master=master, moment_one=moment_one, moment_two=moment_two)


beta_one = 0.9
beta_two = 0.95
learn_rate = 0.001
weight_decay = 0.1
adam_step = 10
epsilon = 1e-08

def adamw(grad, master, moment_one, moment_two):
    first = beta_one * moment_one + (1.0 - beta_one) * grad
    second = beta_two * moment_two + (1.0 - beta_two) * grad * grad
    first_hat = first / (1.0 - beta_one ** adam_step)
    second_hat = second / (1.0 - beta_two ** adam_step)
    updated = master - learn_rate * (first_hat / (jnp.sqrt(second_hat) + epsilon) + weight_decay * master)
    return (updated, first, second)

def reference(activations, value_grads, lengths, master, moment_one, moment_two):
    total_tokens = activations.shape[0]
    width = activations.shape[1]
    columns = value_grads.shape[1]
    index = jnp.arange(total_tokens, dtype=jnp.int32)
    limit = lengths[index // SEQ]
    masked = jnp.where((index % SEQ < limit)[:, None], value_grads, jnp.zeros_like(value_grads))
    weight = master.astype(jnp.bfloat16)
    block = columns // N_TENSOR
    summed = jnp.zeros((total_tokens, width), jnp.float32)
    for head_block in range(N_TENSOR):
        part = jnp.dot(masked[:, head_block * block:(head_block + 1) * block], weight[:, head_block * block:(head_block + 1) * block].T, preferred_element_type=jnp.float32)
        part = lax.optimization_barrier(part.astype(jnp.bfloat16))
        summed = summed + part.astype(jnp.float32)
    input_grads = summed.astype(jnp.bfloat16)
    ranks = N_REPLICA * N_FSDP
    act_blocks = activations.reshape(ranks, TOK_DEV, width)
    grad_blocks = masked.reshape(ranks, TOK_DEV, columns)

    def accumulate(carry, pair):
        term = lax.dot_general(pair[0], pair[1], (((0,), (0,)), ((), ())), preferred_element_type=jnp.float32)
        term = lax.optimization_barrier(term.astype(jnp.bfloat16))
        return (carry + term.astype(jnp.float32), None)
    grad_sum, _ = lax.scan(accumulate, jnp.zeros((width, columns), jnp.float32), (act_blocks, grad_blocks))
    grad = grad_sum / float(total_tokens)
    new_master, new_one, new_two = adamw(grad, master, moment_one, moment_two)
    return (input_grads, new_master, new_one, new_two)
```

```python
import jax
import jax.numpy as jnp
from jax import lax
from jax.sharding import Mesh
from jax.sharding import PartitionSpec as P

AXES = ("za", "zb", "y", "h", "x", "c")
ROWS = ("y", "h")
COLS = ("x", "c")
TOKENS = ("za", "zb", "y", "h")
NEAR = ("zb", "y")

beta_one = 0.9
beta_two = 0.95
learn_rate = 0.001
weight_decay = 0.1
adam_step = 10
epsilon = 1e-08

F32 = jnp.float32
BF16 = jnp.bfloat16


def adamw(grad, master, moment_one, moment_two):
    first = beta_one * moment_one + (1.0 - beta_one) * grad
    second = beta_two * moment_two + (1.0 - beta_two) * grad * grad
    first_hat = first / (1.0 - beta_one**adam_step)
    second_hat = second / (1.0 - beta_two**adam_step)
    updated = master - learn_rate * (
        first_hat / (jnp.sqrt(second_hat) + epsilon) + weight_decay * master
    )
    return (updated, first, second)


def swapped(array, axis, bit=1):
    size = lax.axis_size(axis)
    return lax.ppermute(array, axis, [(k, k ^ bit) for k in range(size)])


def exchanged(pieces, axes):
    return lax.all_to_all(pieces, axes, split_axis=0, concat_axis=0, tiled=True)


def gathered(array, axes):
    count = lax.axis_size(axes)
    return exchanged(jnp.broadcast_to(array[None], (count, *array.shape)), axes)


def own_first(pair, index):
    flip = index == 0
    return jnp.where(flip, pair[0], pair[1]), jnp.where(flip, pair[1], pair[0])


def masked_grads(value_grads, lengths):
    tok_rows = value_grads.shape[0]
    seq_count = lengths.shape[0]
    seq_len = tok_rows // seq_count
    index = jnp.arange(tok_rows, dtype=jnp.int32)
    pick = (index // seq_len)[:, None] == jnp.arange(seq_count, dtype=jnp.int32)[None, :]
    limit = jnp.sum(jnp.where(pick, lengths[None, :], 0), axis=1)
    return jnp.where((index % seq_len < limit)[:, None], value_grads, jnp.zeros_like(value_grads))


def local(activations, value_grads, lengths, master, moment_one, moment_two):
    tok, width = activations.shape
    rows, cols = master.shape
    nzb, ny, nx = lax.axis_size("zb"), lax.axis_size("y"), lax.axis_size("x")
    near = nzb * ny
    shares = lax.axis_size(COLS)
    share = tok // shares
    part = rows // nzb
    h, c, zb = lax.axis_index("h"), lax.axis_index("c"), lax.axis_index("zb")

    weight = master.astype(BF16)
    other_weight = swapped(weight, "h")

    mine = lax.dynamic_slice_in_dim(activations, lax.axis_index(COLS) * share, share, 0)
    mine = mine.reshape(share, ny, 2, nzb, part).transpose(3, 1, 0, 2, 4)
    mine = mine.reshape(near, share, 2 * part)
    act_share = exchanged(mine, NEAR)
    act_own = gathered(act_share, "x")
    act_other = swapped(act_own, "c")

    masked = masked_grads(value_grads, lengths)
    grads = gathered(masked, NEAR)

    by_core = grads.reshape(near, nx, 2, share, cols).transpose(2, 1, 0, 3, 4)
    grads_own, grads_other = own_first((by_core[0], by_core[1]), c)

    def outer(a, g):
        return lax.dot_general(
            a.reshape(-1, 2 * part),
            g.reshape(-1, cols),
            (((0,), (0,)), ((), ())),
            preferred_element_type=F32,
        )

    partial = outer(act_own, grads_own) + outer(act_other, grads_other)
    partial = partial.astype(BF16).reshape(2, part, cols)
    keep, send = own_first((partial[0], partial[1]), h)
    total = (keep.astype(F32) + swapped(send, "h").astype(F32)).astype(BF16)
    for bit in (1, 2):
        if bit < lax.axis_size("za"):
            total = (total.astype(F32) + swapped(total, "za", bit).astype(F32)).astype(BF16)
    grad = gathered(total, "zb").reshape(rows, cols).astype(F32)
    count = float(tok * lax.axis_size(TOKENS))
    new_master, new_one, new_two = adamw(grad / count, master, moment_one, moment_two)

    tokens = lax.dynamic_slice_in_dim(grads, zb * ny, ny, 0).reshape(ny * tok, cols)
    weight_keep, weight_send = own_first((weight, other_weight), h ^ c)

    def product(w):
        return lax.dot_general(
            tokens, w, (((1,), (1,)), ((), ())), preferred_element_type=F32
        )

    sent = swapped(product(weight_send).astype(BF16), "c")
    summed = (product(weight_keep) + sent.astype(F32)).astype(BF16)
    arrived = exchanged(summed.reshape(nx, tok, rows), "x")
    block = arrived.astype(F32).sum(axis=0).astype(BF16)
    turn = [(y * nx + x, x * nx + y) for y in range(ny) for x in range(nx)]
    input_grads = lax.ppermute(block, ("y", "x"), turn)
    return (input_grads, new_master, new_one, new_two)


def solution(mesh):
    replica, fsdp, tensor = (mesh.shape[a] for a in ("replica", "fsdp", "tensor"))
    near = 4 if replica == 16 else 2
    split = Mesh(
        mesh.devices.reshape(replica // near, near, fsdp // 2, 2, tensor // 2, 2), AXES
    )
    in_specs = (
        P(TOKENS, None),
        P(TOKENS, COLS),
        P(TOKENS),
        P(ROWS, COLS),
        P(ROWS, COLS),
        P(ROWS, COLS),
    )
    out_specs = (P(TOKENS, COLS), P(ROWS, COLS), P(ROWS, COLS), P(ROWS, COLS))
    return jax.shard_map(local, mesh=split, in_specs=in_specs, out_specs=out_specs, check_vma=False)
```

```python
import jax
import jax.numpy as jnp
from jax import lax
from jax.sharding import Mesh
from jax.sharding import PartitionSpec as P


AXES = ("za", "zb", "y", "h", "x", "c")
ROWS = ("y", "h")
COLS = ("x", "c")
TOKENS = ("za", "zb", "y", "h")
NEAR = ("zb", "y")

beta_one = 0.9
beta_two = 0.95
learn_rate = 0.001
weight_decay = 0.1
adam_step = 10
epsilon = 1e-08

F32 = jnp.float32
BF16 = jnp.bfloat16


def adamw(grad, master, moment_one, moment_two):
    first = beta_one * moment_one + (1.0 - beta_one) * grad
    second = beta_two * moment_two + (1.0 - beta_two) * grad * grad
    first_hat = first / (1.0 - beta_one**adam_step)
    second_hat = second / (1.0 - beta_two**adam_step)
    updated = master - learn_rate * (
        first_hat / (jnp.sqrt(second_hat) + epsilon) + weight_decay * master
    )
    return (updated, first, second)


def swapped(array, axis, bit=1):
    size = lax.axis_size(axis)
    return lax.ppermute(array, axis, [(k, k ^ bit) for k in range(size)])


def exchanged(pieces, axes):
    return lax.all_to_all(pieces, axes, split_axis=0, concat_axis=0, tiled=True)


def gathered(array, axes):
    count = lax.axis_size(axes)
    return exchanged(jnp.broadcast_to(array[None], (count, *array.shape)), axes)


def across(array):
    count = lax.axis_size("za")
    far = count // 2
    pairs = [(2 * za + h, 2 * (za ^ far) + 1 - h) for za in range(count) for h in range(2)]
    return lax.ppermute(array, ("za", "h"), pairs)


def own_first(pair, index):
    flip = index == 0
    return jnp.where(flip, pair[0], pair[1]), jnp.where(flip, pair[1], pair[0])


def masked_grads(value_grads, lengths):
    tok_rows = value_grads.shape[0]
    seq_count = lengths.shape[0]
    seq_len = tok_rows // seq_count
    index = jnp.arange(tok_rows, dtype=jnp.int32)
    pick = (index // seq_len)[:, None] == jnp.arange(seq_count, dtype=jnp.int32)[None, :]
    limit = jnp.sum(jnp.where(pick, lengths[None, :], 0), axis=1)
    return jnp.where((index % seq_len < limit)[:, None], value_grads, jnp.zeros_like(value_grads))


def step(activations, value_grads, lengths, master, moment_one, moment_two):
    tok, _ = activations.shape
    rows, cols = master.shape
    nzb, ny, nx = lax.axis_size("zb"), lax.axis_size("y"), lax.axis_size("x")
    near = nzb * ny
    shares = lax.axis_size(COLS)
    share = tok // shares
    part = rows // nzb
    h, c, zb = lax.axis_index("h"), lax.axis_index("c"), lax.axis_index("zb")

    weight = lax.dynamic_slice_in_dim(master, zb * part, part, 0).astype(BF16)
    other_weight = across(weight)

    mine = lax.dynamic_slice_in_dim(activations, lax.axis_index(COLS) * share, share, 0)
    mine = mine.reshape(share, ny, 2, nzb, part).transpose(3, 1, 0, 2, 4)
    mine = mine.reshape(near, share, 2 * part)
    act_share = exchanged(mine, NEAR)

    masked = masked_grads(value_grads, lengths)
    copies = jnp.broadcast_to(masked[None], (near, tok, cols))
    copies, act_share = lax.optimization_barrier((copies, act_share))
    grads = exchanged(copies, NEAR)

    x = lax.axis_index("x")
    act_own = jnp.zeros((nx, *act_share.shape), BF16)
    act_own = lax.dynamic_update_index_in_dim(act_own, act_share, x, 0)
    for k in range(1, nx):
        piece = swapped(act_share, "x", k)
        act_own = lax.dynamic_update_index_in_dim(act_own, piece, x ^ k, 0)
    act_other = swapped(act_own, "c")

    tokens = grads.reshape(near * tok, cols)
    weight_keep, weight_send = own_first((weight, other_weight), h ^ c)

    def product(w):
        return lax.dot_general(
            tokens, w, (((1,), (1,)), ((), ())), preferred_element_type=F32
        )

    sent = swapped(product(weight_send).astype(BF16), "c")
    summed = (product(weight_keep) + sent.astype(F32)).astype(BF16)
    arrived = exchanged(summed.reshape(nzb * nx, tok, part), ("zb", "x"))
    block = arrived.astype(F32).reshape(nzb, nx, tok, part).sum(axis=1)
    block = block.transpose(1, 0, 2).reshape(tok, rows).astype(BF16)
    turn = [(y * nx + x, x * nx + y) for y in range(ny) for x in range(nx)]
    input_grads = lax.ppermute(block, ("y", "x"), turn)

    by_core = grads.reshape(near, nx, 2, share, cols).transpose(2, 1, 0, 3, 4)
    grads_own, grads_other = own_first((by_core[0], by_core[1]), c)

    def outer(a, g):
        return lax.dot_general(
            a.reshape(-1, 2 * part),
            g.reshape(-1, cols),
            (((0,), (0,)), ((), ())),
            preferred_element_type=F32,
        )

    partial = outer(act_own, grads_own) + outer(act_other, grads_other)
    partial = partial.astype(BF16).reshape(2, part, cols)
    keep, send = own_first((partial[0], partial[1]), h)
    received = across(send)
    total = (keep.astype(F32) + received.astype(F32)).astype(BF16)
    for bit in (1, 2):
        if bit < lax.axis_size("za"):
            received = swapped(total, "za", bit)
            total = (total.astype(F32) + received.astype(F32)).astype(BF16)
    grad = gathered(total, "zb").reshape(rows, cols).astype(F32)
    count = float(tok * lax.axis_size(TOKENS))
    new_master, new_one, new_two = adamw(grad / count, master, moment_one, moment_two)
    return (input_grads, new_master, new_one, new_two)


def solution(mesh):
    replica, fsdp, tensor = (mesh.shape[a] for a in ("replica", "fsdp", "tensor"))
    near = 4 if replica == 16 else 2
    split = Mesh(
        mesh.devices.reshape(replica // near, near, fsdp // 2, 2, tensor // 2, 2), AXES
    )
    in_specs = (
        P(TOKENS, None),
        P(TOKENS, COLS),
        P(TOKENS),
        P(ROWS, COLS),
        P(ROWS, COLS),
        P(ROWS, COLS),
    )
    out_specs = (P(TOKENS, COLS), P(ROWS, COLS), P(ROWS, COLS), P(ROWS, COLS))
    return jax.shard_map(
        step, mesh=split, in_specs=in_specs, out_specs=out_specs, check_vma=False
    )
```

```python
import functools

import jax
import jax.numpy as jnp
from jax import lax
from jax.experimental import pallas as pl
from jax.experimental.pallas import tpu as pltpu
from jax.sharding import Mesh
from jax.sharding import PartitionSpec as P


AXES = ("za", "zb", "y", "h", "x", "c")
ROWS = ("y", "h")
COLS = ("x", "c")
TOKENS = ("za", "zb", "y", "h")
NEAR = ("zb", "y")

beta_one = 0.9
beta_two = 0.95
learn_rate = 0.001
weight_decay = 0.1
adam_step = 10
epsilon = 1e-08

SMALL = 8 * 2**20

F32 = jnp.float32
BF16 = jnp.bfloat16


def adamw(grad, master, moment_one, moment_two):
    first = beta_one * moment_one + (1.0 - beta_one) * grad
    second = beta_two * moment_two + (1.0 - beta_two) * grad * grad
    first_hat = first / (1.0 - beta_one**adam_step)
    second_hat = second / (1.0 - beta_two**adam_step)
    updated = master - learn_rate * (
        first_hat / (jnp.sqrt(second_hat) + epsilon) + weight_decay * master
    )
    return (updated, first, second)


def swapped(array, axis, bit=1):
    size = lax.axis_size(axis)
    return lax.ppermute(array, axis, [(k, k ^ bit) for k in range(size)])


def exchanged(pieces, axes):
    return lax.all_to_all(pieces, axes, split_axis=0, concat_axis=0, tiled=True)


def gathered(array, axes):
    count = lax.axis_size(axes)
    return exchanged(jnp.broadcast_to(array[None], (count, *array.shape)), axes)


def across(array):
    count = lax.axis_size("za")
    far = count // 2
    pairs = [(2 * za + h, 2 * (za ^ far) + 1 - h) for za in range(count) for h in range(2)]
    return lax.ppermute(array, ("za", "h"), pairs)


def own_first(pair, index):
    flip = index == 0
    return jnp.where(flip, pair[0], pair[1]), jnp.where(flip, pair[1], pair[0])


def masked_grads(value_grads, lengths):
    tok_rows = value_grads.shape[0]
    seq_count = lengths.shape[0]
    seq_len = tok_rows // seq_count
    index = jnp.arange(tok_rows, dtype=jnp.int32)
    pick = (index // seq_len)[:, None] == jnp.arange(seq_count, dtype=jnp.int32)[None, :]
    limit = jnp.sum(jnp.where(pick, lengths[None, :], 0), axis=1)
    return jnp.where((index % seq_len < limit)[:, None], value_grads, jnp.zeros_like(value_grads))


def share_kernel(nzb, where_ref, act_ref, out_ref):
    near, _, width = out_ref.shape
    part = width // 2
    ny = act_ref.shape[1] // (2 * nzb * part)
    h = where_ref[1]
    for k in range(near):
        zb, y = k // ny, k % ny
        for side, half in enumerate((1 - h, h)):
            start = ((y * 2 + half) * nzb + zb) * part
            block = act_ref[:, pl.ds(pl.multiple_of(start, part), part)]
            out_ref[k, :, side * part : (side + 1) * part] = block


def share_of(activations, index, h, nzb, near, share, part):
    return pl.pallas_call(
        functools.partial(share_kernel, nzb),
        out_shape=jax.ShapeDtypeStruct((near, share, 2 * part), activations.dtype),
        grid_spec=pltpu.PrefetchScalarGridSpec(
            num_scalar_prefetch=1,
            grid=(1,),
            in_specs=[pl.BlockSpec((share, activations.shape[1]), lambda i, where: (where[0], 0))],
            out_specs=pl.BlockSpec((near, share, 2 * part), lambda i, where: (0, 0, 0)),
        ),
        name="share",
    )(jnp.stack([index, h]).astype(jnp.int32), activations)


def outer_kernel(half, x_ref, *refs):
    *pieces, grads_ref, out_ref = refs
    near, tok, _ = grads_ref.shape
    share = tok // len(pieces)
    cols = out_ref.shape[1]
    total = None
    for k, piece in enumerate(pieces):
        start = pl.multiple_of((x_ref[0] ^ k) * share, share)
        grads = grads_ref[:, pl.ds(start, share), half * cols : (half + 1) * cols]
        term = lax.dot_general(
            piece[...],
            grads.reshape(near * share, cols),
            (((0,), (0,)), ((), ())),
            preferred_element_type=F32,
        )
        total = term if total is None else total + term
    out_ref[...] = total.astype(out_ref.dtype)


def outer(x, pieces, grads, half, dtype):
    rows, cols = pieces[0].shape[1], grads.shape[2] // 2
    vmem = pl.BlockSpec(memory_space=pltpu.VMEM)
    depth = grads.shape[0] * grads.shape[1]
    return pl.pallas_call(
        functools.partial(outer_kernel, half),
        out_shape=jax.ShapeDtypeStruct((rows, cols), dtype),
        in_specs=[pl.BlockSpec(memory_space=pltpu.SMEM)] + [vmem] * (len(pieces) + 1),
        out_specs=vmem,
        cost_estimate=pl.CostEstimate(
            flops=2 * depth * rows * cols,
            bytes_accessed=2 * depth * (rows + cols),
            transcendentals=0,
        ),
        compiler_params=pltpu.CompilerParams(vmem_limit_bytes=SMALL),
    )(x.reshape(1), *pieces, grads)


def step(activations, value_grads, lengths, master, moment_one, moment_two):
    tok, _ = activations.shape
    rows, cols = master.shape
    nzb, ny, nx = lax.axis_size("zb"), lax.axis_size("y"), lax.axis_size("x")
    near = nzb * ny
    half = tok // 2
    share = half // nx
    part = rows // nzb
    h, c, zb = lax.axis_index("h"), lax.axis_index("c"), lax.axis_index("zb")
    x = lax.axis_index("x")

    masked = masked_grads(value_grads, lengths)
    vg_own, vg_send = own_first((masked[:half], masked[half:]), c)
    vg_other = swapped(vg_send, "c")
    vg_half = jnp.concatenate([vg_own, vg_other], axis=1)

    weight = lax.dynamic_slice_in_dim(master, zb * part, part, 0).astype(BF16)
    weight_far = across(weight)

    mine = share_of(activations, c * nx + x, h, nzb, near, share, part)
    act_share = exchanged(mine, NEAR)
    copies = jnp.broadcast_to(vg_half[None], (near, half, 2 * cols))
    copies, act_share = lax.optimization_barrier((copies, act_share))
    grads = exchanged(copies, NEAR)
    act_share = act_share.reshape(near * share, 2 * part)
    pieces = [act_share]
    for k in range(1, nx):
        pieces.append(swapped(act_share, "x", k))

    partial = outer(x, pieces, grads, 1, BF16)
    partial = swapped(partial, "c")
    partial = outer(x, pieces, grads, 0, F32) + partial.astype(F32)
    received = across(partial[:part].astype(BF16))
    total = (partial[part:] + received.astype(F32)).astype(BF16)
    for bit in (1, 2):
        if bit < lax.axis_size("za"):
            received = swapped(total, "za", bit)
            total = (total.astype(F32) + received.astype(F32)).astype(BF16)
    grad = gathered(total, "zb").reshape(rows, cols).astype(F32)
    count = float(tok * lax.axis_size(TOKENS))
    new_master, new_one, new_two = adamw(grad / count, master, moment_one, moment_two)

    both = jnp.concatenate(own_first((weight, weight_far), h), axis=0)
    both_other = swapped(both, "c")
    both = jnp.concatenate([both, both_other], axis=1)
    tokens = grads.reshape(near * half, 2 * cols)

    def product(w):
        out = lax.dot_general(tokens, w, (((1,), (1,)), ((), ())), preferred_element_type=F32)
        return out.astype(BF16).reshape(nzb, ny, half, part).transpose(1, 0, 2, 3)

    product = jnp.stack([product(both[:part]), product(both[part:])], axis=1)
    arrived = exchanged(product.reshape(ny * 2, nzb * half, part), COLS)
    block = arrived.reshape(nx, 2, nzb, half, part).astype(F32).sum(axis=0).astype(BF16)
    block = block.transpose(1, 0, 2, 3).reshape(nzb, tok, part)
    block = exchanged(block, "zb")
    block = block.transpose(1, 0, 2).reshape(tok, rows)
    turn = [(y * nx + x, x * nx + y) for y in range(ny) for x in range(nx)]
    input_grads = lax.ppermute(block, ("y", "x"), turn)
    return (input_grads, new_master, new_one, new_two)


def solution(mesh):
    replica, fsdp, tensor = (mesh.shape[a] for a in ("replica", "fsdp", "tensor"))
    near = 4 if replica == 16 else 2
    split = Mesh(
        mesh.devices.reshape(replica // near, near, fsdp // 2, 2, tensor // 2, 2), AXES
    )
    in_specs = (
        P(TOKENS, None),
        P(TOKENS, COLS),
        P(TOKENS),
        P(ROWS, COLS),
        P(ROWS, COLS),
        P(ROWS, COLS),
    )
    out_specs = (P(TOKENS, COLS), P(ROWS, COLS), P(ROWS, COLS), P(ROWS, COLS))
    return jax.shard_map(step, mesh=split, in_specs=in_specs, out_specs=out_specs, check_vma=False)
```

```python
import functools

import jax
import jax.numpy as jnp
from jax import lax
from jax.experimental import pallas as pl
from jax.experimental.pallas import tpu as pltpu
from jax.sharding import Mesh
from jax.sharding import PartitionSpec as P


AXES = ("za", "zb", "y", "h", "x", "c")
ROWS = ("y", "h")
COLS = ("x", "c")
TOKENS = ("za", "zb", "y", "h")
NEAR = ("zb", "y")

beta_one = 0.9
beta_two = 0.95
learn_rate = 0.001
weight_decay = 0.1
adam_step = 10
epsilon = 1e-08

SMALL = 8 * 2**20

F32 = jnp.float32
BF16 = jnp.bfloat16


def adamw(grad, master, moment_one, moment_two):
    first = beta_one * moment_one + (1.0 - beta_one) * grad
    second = beta_two * moment_two + (1.0 - beta_two) * grad * grad
    first_hat = first / (1.0 - beta_one**adam_step)
    second_hat = second / (1.0 - beta_two**adam_step)
    updated = master - learn_rate * (
        first_hat / (jnp.sqrt(second_hat) + epsilon) + weight_decay * master
    )
    return (updated, first, second)


def swapped(array, axis, bit=1):
    size = lax.axis_size(axis)
    return lax.ppermute(array, axis, [(k, k ^ bit) for k in range(size)])


def exchanged(pieces, axes):
    return lax.all_to_all(pieces, axes, split_axis=0, concat_axis=0, tiled=True)


def gathered(array, axes):
    count = lax.axis_size(axes)
    return exchanged(jnp.broadcast_to(array[None], (count, *array.shape)), axes)


def across(array):
    count = lax.axis_size("za")
    far = count // 2
    pairs = [(2 * za + h, 2 * (za ^ far) + 1 - h) for za in range(count) for h in range(2)]
    return lax.ppermute(array, ("za", "h"), pairs)


def own_first(pair, index):
    flip = index == 0
    return jnp.where(flip, pair[0], pair[1]), jnp.where(flip, pair[1], pair[0])


def masked_grads(value_grads, lengths):
    tok_rows = value_grads.shape[0]
    seq_count = lengths.shape[0]
    seq_len = tok_rows // seq_count
    index = jnp.arange(tok_rows, dtype=jnp.int32)
    pick = (index // seq_len)[:, None] == jnp.arange(seq_count, dtype=jnp.int32)[None, :]
    limit = jnp.sum(jnp.where(pick, lengths[None, :], 0), axis=1)
    return jnp.where((index % seq_len < limit)[:, None], value_grads, jnp.zeros_like(value_grads))


def share_kernel(nzb, where_ref, act_ref, out_ref):
    near, _, width = out_ref.shape
    part = width // 2
    ny = act_ref.shape[1] // (2 * nzb * part)
    h = where_ref[1]
    for k in range(near):
        zb, y = k // ny, k % ny
        for side, half in enumerate((1 - h, h)):
            start = ((y * 2 + half) * nzb + zb) * part
            block = act_ref[:, pl.ds(pl.multiple_of(start, part), part)]
            out_ref[k, :, side * part : (side + 1) * part] = block


def share_of(activations, index, h, nzb, near, share, part):
    return pl.pallas_call(
        functools.partial(share_kernel, nzb),
        out_shape=jax.ShapeDtypeStruct((near, share, 2 * part), activations.dtype),
        grid_spec=pltpu.PrefetchScalarGridSpec(
            num_scalar_prefetch=1,
            grid=(1,),
            in_specs=[pl.BlockSpec((share, activations.shape[1]), lambda i, where: (where[0], 0))],
            out_specs=pl.BlockSpec((near, share, 2 * part), lambda i, where: (0, 0, 0)),
        ),
        name="share",
    )(jnp.stack([index, h]).astype(jnp.int32), activations)


def outer_kernel(half, x_ref, *refs):
    *pieces, grads_ref, out_ref = refs
    ny, nzb, tok, _ = grads_ref.shape
    share = tok // len(pieces)
    cols = out_ref.shape[1]
    total = None
    for k, piece in enumerate(pieces):
        start = pl.multiple_of((x_ref[0] ^ k) * share, share)
        grads = [
            grads_ref[y, zb, pl.ds(start, share), half * cols : (half + 1) * cols]
            for zb in range(nzb)
            for y in range(ny)
        ]
        term = lax.dot_general(
            piece[...],
            jnp.concatenate(grads, axis=0),
            (((0,), (0,)), ((), ())),
            preferred_element_type=F32,
        )
        total = term if total is None else total + term
    out_ref[...] = total.astype(out_ref.dtype)


def outer(x, pieces, grads, half, dtype):
    rows, cols = pieces[0].shape[1], grads.shape[3] // 2
    vmem = pl.BlockSpec(memory_space=pltpu.VMEM)
    depth = sum(piece.shape[0] for piece in pieces)
    return pl.pallas_call(
        functools.partial(outer_kernel, half),
        out_shape=jax.ShapeDtypeStruct((rows, cols), dtype),
        in_specs=[pl.BlockSpec(memory_space=pltpu.SMEM)] + [vmem] * (len(pieces) + 1),
        out_specs=vmem,
        cost_estimate=pl.CostEstimate(
            flops=2 * depth * rows * cols,
            bytes_accessed=2 * depth * (rows + cols),
            transcendentals=0,
        ),
        compiler_params=pltpu.CompilerParams(vmem_limit_bytes=SMALL),
    )(x.reshape(1), *pieces, grads)


def step(activations, value_grads, lengths, master, moment_one, moment_two):
    tok, _ = activations.shape
    rows, cols = master.shape
    nzb, ny, nx = lax.axis_size("zb"), lax.axis_size("y"), lax.axis_size("x")
    near = nzb * ny
    half = tok // 2
    share = half // nx
    part = rows // nzb
    h, c, zb = lax.axis_index("h"), lax.axis_index("c"), lax.axis_index("zb")
    x = lax.axis_index("x")

    masked = masked_grads(value_grads, lengths)
    vg_own, vg_send = own_first((masked[:half], masked[half:]), c)
    vg_other = swapped(vg_send, "c")
    vg_half = jnp.concatenate([vg_own, vg_other], axis=1)
    vg_near = gathered(vg_half, "zb").reshape(nzb * half, 2 * cols)

    weight = lax.dynamic_slice_in_dim(master, zb * part, part, 0).astype(BF16)
    weight_far = across(weight)

    mine = share_of(activations, c * nx + x, h, nzb, near, share, part)
    act_share = exchanged(mine, NEAR)
    copies = jnp.broadcast_to(vg_near[None], (ny, nzb * half, 2 * cols))
    copies, act_share = lax.optimization_barrier((copies, act_share))
    grads = exchanged(copies, "y").reshape(ny, nzb, half, 2 * cols)
    act_share = act_share.reshape(near * share, 2 * part)
    pieces = [act_share]
    for k in range(1, nx):
        pieces.append(swapped(act_share, "x", k))

    partial = outer(x, pieces, grads, 1, BF16)
    partial = swapped(partial, "c")
    partial = outer(x, pieces, grads, 0, F32) + partial.astype(F32)
    received = across(partial[:part].astype(BF16))
    total = (partial[part:] + received.astype(F32)).astype(BF16)
    for bit in (1, 2):
        if bit < lax.axis_size("za"):
            received = swapped(total, "za", bit)
            total = (total.astype(F32) + received.astype(F32)).astype(BF16)
    grad = gathered(total, "zb").reshape(rows, cols).astype(F32)
    count = float(tok * lax.axis_size(TOKENS))
    new_master, new_one, new_two = adamw(grad / count, master, moment_one, moment_two)

    both = jnp.concatenate(own_first((weight, weight_far), h), axis=0)
    both_other = swapped(both, "c")
    both = jnp.concatenate([both, both_other], axis=1)
    tokens = grads.reshape(near * half, 2 * cols)

    def product(w):
        out = lax.dot_general(tokens, w, (((1,), (1,)), ((), ())), preferred_element_type=F32)
        return out.astype(BF16).reshape(ny, nzb, half, part)

    product = jnp.stack([product(both[:part]), product(both[part:])], axis=1)
    arrived = exchanged(product.reshape(ny * 2, nzb * half, part), COLS)
    block = arrived.reshape(nx, 2, nzb, half, part).astype(F32).sum(axis=0).astype(BF16)
    block = block.transpose(1, 0, 2, 3).reshape(nzb, tok, part)
    block = exchanged(block, "zb")
    block = block.transpose(1, 0, 2).reshape(tok, rows)
    turn = [(y * nx + x, x * nx + y) for y in range(ny) for x in range(nx)]
    input_grads = lax.ppermute(block, ("y", "x"), turn)
    return (input_grads, new_master, new_one, new_two)


def solution(mesh):
    replica, fsdp, tensor = (mesh.shape[a] for a in ("replica", "fsdp", "tensor"))
    near = 4 if replica == 16 else 2
    split = Mesh(
        mesh.devices.reshape(replica // near, near, fsdp // 2, 2, tensor // 2, 2), AXES
    )
    in_specs = (
        P(TOKENS, None),
        P(TOKENS, COLS),
        P(TOKENS),
        P(ROWS, COLS),
        P(ROWS, COLS),
        P(ROWS, COLS),
    )
    out_specs = (P(TOKENS, COLS), P(ROWS, COLS), P(ROWS, COLS), P(ROWS, COLS))
    return jax.shard_map(step, mesh=split, in_specs=in_specs, out_specs=out_specs, check_vma=False)
```

```python
import functools

import jax
import jax.numpy as jnp
from jax import lax
from jax.experimental import pallas as pl
from jax.experimental.pallas import tpu as pltpu
from jax.sharding import Mesh
from jax.sharding import PartitionSpec as P


AXES = ("za", "zb", "y", "h", "x", "c")
ROWS = ("y", "h")
COLS = ("x", "c")
TOKENS = ("za", "zb", "y", "h")

beta_one = 0.9
beta_two = 0.95
learn_rate = 0.001
weight_decay = 0.1
adam_step = 10
epsilon = 1e-08

SMALL = 8 * 2**20

F32 = jnp.float32
BF16 = jnp.bfloat16


def adamw(grad, master, moment_one, moment_two):
    first = beta_one * moment_one + (1.0 - beta_one) * grad
    second = beta_two * moment_two + (1.0 - beta_two) * grad * grad
    first_hat = first / (1.0 - beta_one**adam_step)
    second_hat = second / (1.0 - beta_two**adam_step)
    updated = master - learn_rate * (
        first_hat / (jnp.sqrt(second_hat) + epsilon) + weight_decay * master
    )
    return (updated, first, second)


def swapped(array, axis, bit=1):
    size = lax.axis_size(axis)
    return lax.ppermute(array, axis, [(k, k ^ bit) for k in range(size)])


def exchanged(pieces, axes):
    return lax.all_to_all(pieces, axes, split_axis=0, concat_axis=0, tiled=True)


def gathered(array, axes):
    count = lax.axis_size(axes)
    return exchanged(jnp.broadcast_to(array[None], (count, *array.shape)), axes)


def across(array):
    count = lax.axis_size("za")
    far = count // 2
    pairs = [(2 * za + h, 2 * (za ^ far) + 1 - h) for za in range(count) for h in range(2)]
    return lax.ppermute(array, ("za", "h"), pairs)


def own_first(pair, index):
    flip = index == 0
    return jnp.where(flip, pair[0], pair[1]), jnp.where(flip, pair[1], pair[0])


def share_kernel(nzb, seq_len, where_ref, lengths_ref, act_ref, own_ref, other_ref, out_ref):
    _, height, width = out_ref.shape
    share, half, part = act_ref.shape[0], own_ref.shape[0], width // 2
    ny = (height - half) // share
    h, c = where_ref[1], where_ref[2]
    index = c * half + lax.broadcasted_iota(jnp.int32, (half, part), 0)
    live = None
    for k in range(lengths_ref.shape[0]):
        inside = (index >= k * seq_len) & (index < k * seq_len + lengths_ref[k])
        live = inside if live is None else live | inside
    for zb in range(nzb):
        for y in range(ny):
            for side, far in enumerate((1 - h, h)):
                start = ((y * 2 + far) * nzb + zb) * part
                block = act_ref[:, pl.ds(pl.multiple_of(start, part), part)]
                out_ref[zb, y * share : (y + 1) * share, side * part : (side + 1) * part] = block
    for side, ref in enumerate((own_ref, other_ref)):
        block = ref[...].astype(F32)
        block = jnp.where(live, block, jnp.zeros_like(block)).astype(out_ref.dtype)
        for zb in range(nzb):
            out_ref[zb, ny * share :, side * part : (side + 1) * part] = block


def near_pieces(where, lengths, activations, value_grads, other, nzb, ny, share):
    tok, width = activations.shape
    half, cols = other.shape
    shape = (nzb, ny * share + half, 2 * cols)
    return pl.pallas_call(
        functools.partial(share_kernel, nzb, tok // lengths.shape[0]),
        out_shape=jax.ShapeDtypeStruct(shape, activations.dtype),
        grid_spec=pltpu.PrefetchScalarGridSpec(
            num_scalar_prefetch=2,
            grid=(1,),
            in_specs=[
                pl.BlockSpec((share, width), lambda i, where, lengths: (where[0], 0)),
                pl.BlockSpec((half, cols), lambda i, where, lengths: (where[2], 0)),
                pl.BlockSpec((half, cols), lambda i, where, lengths: (0, 0)),
            ],
            out_specs=pl.BlockSpec(shape, lambda i, where, lengths: (0, 0, 0)),
        ),
        name="share",
    )(where, lengths, activations, value_grads, other)


def outer_kernel(half, x_ref, *refs):
    *pieces, grads_ref, out_ref = refs
    ny, nzb, tok, _ = grads_ref.shape
    share = tok // len(pieces)
    cols = out_ref.shape[1]
    total = None
    for k, piece in enumerate(pieces):
        start = pl.multiple_of((x_ref[0] ^ k) * share, share)
        grads = [
            grads_ref[y, zb, pl.ds(start, share), half * cols : (half + 1) * cols]
            for y in range(ny)
            for zb in range(nzb)
        ]
        term = lax.dot_general(
            piece[...],
            jnp.concatenate(grads, axis=0),
            (((0,), (0,)), ((), ())),
            preferred_element_type=F32,
        )
        total = term if total is None else total + term
    out_ref[...] = total.astype(out_ref.dtype)


def outer(x, pieces, grads, half, dtype):
    rows, cols = pieces[0].shape[1], grads.shape[3] // 2
    vmem = pl.BlockSpec(memory_space=pltpu.VMEM)
    depth = sum(piece.shape[0] for piece in pieces)
    return pl.pallas_call(
        functools.partial(outer_kernel, half),
        out_shape=jax.ShapeDtypeStruct((rows, cols), dtype),
        in_specs=[pl.BlockSpec(memory_space=pltpu.SMEM)] + [vmem] * (len(pieces) + 1),
        out_specs=vmem,
        cost_estimate=pl.CostEstimate(
            flops=2 * depth * rows * cols,
            bytes_accessed=2 * depth * (rows + cols),
            transcendentals=0,
        ),
        compiler_params=pltpu.CompilerParams(vmem_limit_bytes=SMALL),
    )(x.reshape(1), *pieces, grads)


def step(activations, value_grads, lengths, master, moment_one, moment_two):
    tok, _ = activations.shape
    rows, cols = master.shape
    nzb, ny, nx = lax.axis_size("zb"), lax.axis_size("y"), lax.axis_size("x")
    near = nzb * ny
    half = tok // 2
    share = half // nx
    part = rows // nzb
    h, c, zb = lax.axis_index("h"), lax.axis_index("c"), lax.axis_index("zb")
    x = lax.axis_index("x")

    send = lax.dynamic_slice_in_dim(value_grads, (1 - c) * half, half, 0)
    vg_other = swapped(send, "c")

    weight = lax.dynamic_slice_in_dim(master, zb * part, part, 0).astype(BF16)
    weight_far = across(weight)

    where = jnp.stack([c * nx + x, h, c]).astype(jnp.int32)
    mine = near_pieces(where, lengths, activations, value_grads, vg_other, nzb, ny, share)
    arrived = exchanged(mine, "zb")
    mine = arrived[:, : ny * share].reshape(nzb, ny, share, 2 * part).transpose(1, 0, 2, 3)
    act_share = exchanged(mine.reshape(ny, nzb * share, 2 * part), "y")
    copies = arrived[:, ny * share :].reshape(nzb * half, 2 * cols)
    copies = jnp.broadcast_to(copies[None], (ny, nzb * half, 2 * cols))
    copies, act_share = lax.optimization_barrier((copies, act_share))
    grads = exchanged(copies, "y").reshape(ny, nzb, half, 2 * cols)
    act_share = act_share.reshape(near * share, 2 * part)
    pieces = [act_share]
    for k in range(1, nx):
        pieces.append(swapped(act_share, "x", k))

    partial = outer(x, pieces, grads, 1, BF16)
    partial = swapped(partial, "c")
    partial = outer(x, pieces, grads, 0, F32) + partial.astype(F32)
    received = across(partial[:part].astype(BF16))
    total = (partial[part:] + received.astype(F32)).astype(BF16)
    for bit in (1, 2):
        if bit < lax.axis_size("za"):
            received = swapped(total, "za", bit)
            total = (total.astype(F32) + received.astype(F32)).astype(BF16)
    grad = gathered(total, "zb").reshape(rows, cols).astype(F32)
    count = float(tok * lax.axis_size(TOKENS))
    new_master, new_one, new_two = adamw(grad / count, master, moment_one, moment_two)

    both = jnp.concatenate(own_first((weight, weight_far), h), axis=0)
    both_other = swapped(both, "c")
    both = jnp.concatenate([both, both_other], axis=1)
    tokens = grads.reshape(near * half, 2 * cols)

    def product(w):
        out = lax.dot_general(tokens, w, (((1,), (1,)), ((), ())), preferred_element_type=F32)
        return out.astype(BF16).reshape(ny, nzb, half, part)

    product = jnp.stack([product(both[:part]), product(both[part:])], axis=1)
    arrived = exchanged(product.reshape(ny * 2, nzb * half, part), COLS)
    block = arrived.reshape(nx, 2, nzb, half, part).astype(F32).sum(axis=0).astype(BF16)
    block = block.transpose(1, 0, 2, 3).reshape(nzb, tok, part)
    block = exchanged(block, "zb")
    block = block.transpose(1, 0, 2).reshape(tok, rows)
    turn = [(y * nx + x, x * nx + y) for y in range(ny) for x in range(nx)]
    input_grads = lax.ppermute(block, ("y", "x"), turn)
    return (input_grads, new_master, new_one, new_two)


def solution(mesh):
    replica, fsdp, tensor = (mesh.shape[a] for a in ("replica", "fsdp", "tensor"))
    near = 4 if replica == 16 else 2
    split = Mesh(
        mesh.devices.reshape(replica // near, near, fsdp // 2, 2, tensor // 2, 2), AXES
    )
    in_specs = (
        P(TOKENS, None),
        P(TOKENS, COLS),
        P(TOKENS),
        P(ROWS, COLS),
        P(ROWS, COLS),
        P(ROWS, COLS),
    )
    out_specs = (P(TOKENS, COLS), P(ROWS, COLS), P(ROWS, COLS), P(ROWS, COLS))
    return jax.shard_map(step, mesh=split, in_specs=in_specs, out_specs=out_specs, check_vma=False)
```

```python
import functools

import jax
import jax.numpy as jnp
from jax import lax
from jax.experimental import pallas as pl
from jax.experimental.pallas import tpu as pltpu
from jax.sharding import Mesh
from jax.sharding import PartitionSpec as P


AXES = ("za", "zb", "y", "h", "x", "c")
ROWS = ("y", "h")
COLS = ("x", "c")
TOKENS = ("za", "zb", "y", "h")
NEAR = ("zb", "y")

beta_one = 0.9
beta_two = 0.95
learn_rate = 0.001
weight_decay = 0.1
adam_step = 10
epsilon = 1e-08

SMALL = 8 * 2**20

F32 = jnp.float32
BF16 = jnp.bfloat16


def adamw(grad, master, moment_one, moment_two):
    first = beta_one * moment_one + (1.0 - beta_one) * grad
    second = beta_two * moment_two + (1.0 - beta_two) * grad * grad
    first_hat = first / (1.0 - beta_one**adam_step)
    second_hat = second / (1.0 - beta_two**adam_step)
    updated = master - learn_rate * (
        first_hat / (jnp.sqrt(second_hat) + epsilon) + weight_decay * master
    )
    return (updated, first, second)


def swapped(array, axis, bit=1):
    size = lax.axis_size(axis)
    return lax.ppermute(array, axis, [(k, k ^ bit) for k in range(size)])


def exchanged(pieces, axes):
    return lax.all_to_all(pieces, axes, split_axis=0, concat_axis=0, tiled=True)


def gathered(array, axes):
    count = lax.axis_size(axes)
    return exchanged(jnp.broadcast_to(array[None], (count, *array.shape)), axes)


def across(array):
    count = lax.axis_size("za")
    far = count // 2
    pairs = [(2 * za + h, 2 * (za ^ far) + 1 - h) for za in range(count) for h in range(2)]
    return lax.ppermute(array, ("za", "h"), pairs)


def own_first(pair, index):
    flip = index == 0
    return jnp.where(flip, pair[0], pair[1]), jnp.where(flip, pair[1], pair[0])


def share_kernel(
    nzb, seq_len, where_ref, lengths_ref, act_ref, own_ref, other_ref, mine_ref, copies_ref
):
    near, _, width = mine_ref.shape
    half, part = own_ref.shape[0], width // 2
    cols = own_ref.shape[1]
    ny = near // nzb
    h, c = where_ref[1], where_ref[2]
    for k in range(near):
        zb, y = k // ny, k % ny
        for side, far in enumerate((1 - h, h)):
            start = ((y * 2 + far) * nzb + zb) * part
            block = act_ref[:, pl.ds(pl.multiple_of(start, part), part)]
            mine_ref[k, :, side * part : (side + 1) * part] = block
    index = c * half + lax.broadcasted_iota(jnp.int32, (half, cols), 0)
    live = None
    for k in range(lengths_ref.shape[0]):
        inside = (index >= k * seq_len) & (index < k * seq_len + lengths_ref[k])
        live = inside if live is None else live | inside
    for side, ref in enumerate((own_ref, other_ref)):
        block = ref[...].astype(F32)
        block = jnp.where(live, block, jnp.zeros_like(block)).astype(copies_ref.dtype)
        for k in range(near):
            copies_ref[k, :, side * cols : (side + 1) * cols] = block


def near_pieces(where, lengths, activations, value_grads, other, nzb, ny, share, part):
    tok, width = activations.shape
    half, cols = other.shape
    shapes = ((nzb * ny, share, 2 * part), (nzb * ny, half, 2 * cols))
    return pl.pallas_call(
        functools.partial(share_kernel, nzb, tok // lengths.shape[0]),
        out_shape=[jax.ShapeDtypeStruct(shape, activations.dtype) for shape in shapes],
        grid_spec=pltpu.PrefetchScalarGridSpec(
            num_scalar_prefetch=2,
            grid=(1,),
            in_specs=[
                pl.BlockSpec((share, width), lambda i, where, lengths: (where[0], 0)),
                pl.BlockSpec((half, cols), lambda i, where, lengths: (where[2], 0)),
                pl.BlockSpec((half, cols), lambda i, where, lengths: (0, 0)),
            ],
            out_specs=[pl.BlockSpec(shape, lambda i, where, lengths: (0, 0, 0)) for shape in shapes],
        ),
        name="share",
    )(where, lengths, activations, value_grads, other)


def outer_kernel(half, x_ref, *refs):
    *pieces, grads_ref, out_ref = refs
    near, tok, _ = grads_ref.shape
    share = tok // len(pieces)
    cols = out_ref.shape[1]
    total = None
    for k, piece in enumerate(pieces):
        start = pl.multiple_of((x_ref[0] ^ k) * share, share)
        grads = grads_ref[:, pl.ds(start, share), half * cols : (half + 1) * cols]
        term = lax.dot_general(
            piece[...],
            grads.reshape(near * share, cols),
            (((0,), (0,)), ((), ())),
            preferred_element_type=F32,
        )
        total = term if total is None else total + term
    out_ref[...] = total.astype(out_ref.dtype)


def outer(x, pieces, grads, half, dtype):
    rows, cols = pieces[0].shape[1], grads.shape[2] // 2
    vmem = pl.BlockSpec(memory_space=pltpu.VMEM)
    depth = sum(piece.shape[0] for piece in pieces)
    return pl.pallas_call(
        functools.partial(outer_kernel, half),
        out_shape=jax.ShapeDtypeStruct((rows, cols), dtype),
        in_specs=[pl.BlockSpec(memory_space=pltpu.SMEM)] + [vmem] * (len(pieces) + 1),
        out_specs=vmem,
        cost_estimate=pl.CostEstimate(
            flops=2 * depth * rows * cols,
            bytes_accessed=2 * depth * (rows + cols),
            transcendentals=0,
        ),
        compiler_params=pltpu.CompilerParams(vmem_limit_bytes=SMALL),
    )(x.reshape(1), *pieces, grads)


def step(activations, value_grads, lengths, master, moment_one, moment_two):
    tok, _ = activations.shape
    rows, cols = master.shape
    nzb, ny, nx = lax.axis_size("zb"), lax.axis_size("y"), lax.axis_size("x")
    near = nzb * ny
    half = tok // 2
    share = half // nx
    part = rows // nzb
    h, c, zb = lax.axis_index("h"), lax.axis_index("c"), lax.axis_index("zb")
    x = lax.axis_index("x")

    send = lax.dynamic_slice_in_dim(value_grads, (1 - c) * half, half, 0)
    vg_other = swapped(send, "c")

    weight = lax.dynamic_slice_in_dim(master, zb * part, part, 0).astype(BF16)
    weight_far = across(weight)

    where = jnp.stack([c * nx + x, h, c]).astype(jnp.int32)
    mine, copies = near_pieces(
        where, lengths, activations, value_grads, vg_other, nzb, ny, share, part
    )
    act_share = exchanged(mine, NEAR)
    copies, act_share = lax.optimization_barrier((copies, act_share))
    grads = exchanged(copies, NEAR)
    act_share = act_share.reshape(near * share, 2 * part)
    pieces = [act_share]
    for k in range(1, nx):
        pieces.append(swapped(act_share, "x", k))

    partial = outer(x, pieces, grads, 1, BF16)
    partial = swapped(partial, "c")
    partial = outer(x, pieces, grads, 0, F32) + partial.astype(F32)
    received = across(partial[:part].astype(BF16))
    total = (partial[part:] + received.astype(F32)).astype(BF16)
    for bit in (1, 2):
        if bit < lax.axis_size("za"):
            received = swapped(total, "za", bit)
            total = (total.astype(F32) + received.astype(F32)).astype(BF16)
    grad = gathered(total, "zb").reshape(rows, cols).astype(F32)
    count = float(tok * lax.axis_size(TOKENS))
    new_master, new_one, new_two = adamw(grad / count, master, moment_one, moment_two)

    both = jnp.concatenate(own_first((weight, weight_far), h), axis=0)
    both_other = swapped(both, "c")
    both = jnp.concatenate([both, both_other], axis=1)
    tokens = grads.reshape(near * half, 2 * cols)

    def product(w):
        out = lax.dot_general(tokens, w, (((1,), (1,)), ((), ())), preferred_element_type=F32)
        return out.astype(BF16).reshape(nzb, ny, half, part).transpose(1, 0, 2, 3)

    product = jnp.stack([product(both[:part]), product(both[part:])], axis=1)
    arrived = exchanged(product.reshape(ny * 2, nzb * half, part), COLS)
    block = arrived.reshape(nx, 2, nzb, half, part).astype(F32).sum(axis=0).astype(BF16)
    block = block.transpose(1, 0, 2, 3).reshape(nzb, tok, part)
    block = exchanged(block, "zb")
    block = block.transpose(1, 0, 2).reshape(tok, rows)
    turn = [(y * nx + x, x * nx + y) for y in range(ny) for x in range(nx)]
    input_grads = lax.ppermute(block, ("y", "x"), turn)
    return (input_grads, new_master, new_one, new_two)


def solution(mesh):
    replica, fsdp, tensor = (mesh.shape[a] for a in ("replica", "fsdp", "tensor"))
    near = 4 if replica == 16 else 2
    split = Mesh(
        mesh.devices.reshape(replica // near, near, fsdp // 2, 2, tensor // 2, 2), AXES
    )
    in_specs = (
        P(TOKENS, None),
        P(TOKENS, COLS),
        P(TOKENS),
        P(ROWS, COLS),
        P(ROWS, COLS),
        P(ROWS, COLS),
    )
    out_specs = (P(TOKENS, COLS), P(ROWS, COLS), P(ROWS, COLS), P(ROWS, COLS))
    return jax.shard_map(
        step, mesh=split, in_specs=in_specs, out_specs=out_specs, check_vma=False
    )
```

```python
import functools

import jax
import jax.numpy as jnp
from jax import lax
from jax.experimental import pallas as pl
from jax.experimental.pallas import tpu as pltpu
from jax.sharding import Mesh
from jax.sharding import PartitionSpec as P


AXES = ("za", "zb", "y", "h", "x", "c")
ROWS = ("y", "h")
COLS = ("x", "c")
TOKENS = ("za", "zb", "y", "h")
NEAR = ("zb", "y")

beta_one = 0.9
beta_two = 0.95
learn_rate = 0.001
weight_decay = 0.1
adam_step = 10
epsilon = 1e-08

SMALL = 8 * 2**20

F32 = jnp.float32
BF16 = jnp.bfloat16


def adamw(grad, master, moment_one, moment_two):
    first = beta_one * moment_one + (1.0 - beta_one) * grad
    second = beta_two * moment_two + (1.0 - beta_two) * grad * grad
    first_hat = first / (1.0 - beta_one**adam_step)
    second_hat = second / (1.0 - beta_two**adam_step)
    updated = master - learn_rate * (
        first_hat / (jnp.sqrt(second_hat) + epsilon) + weight_decay * master
    )
    return (updated, first, second)


def swapped(array, axis, bit=1):
    size = lax.axis_size(axis)
    return lax.ppermute(array, axis, [(k, k ^ bit) for k in range(size)])


def exchanged(pieces, axes):
    return lax.all_to_all(pieces, axes, split_axis=0, concat_axis=0, tiled=True)


def gathered(array, axes):
    count = lax.axis_size(axes)
    return exchanged(jnp.broadcast_to(array[None], (count, *array.shape)), axes)


def across(array):
    count = lax.axis_size("za")
    far = count // 2
    pairs = [(2 * za + h, 2 * (za ^ far) + 1 - h) for za in range(count) for h in range(2)]
    return lax.ppermute(array, ("za", "h"), pairs)


def own_first(pair, index):
    flip = index == 0
    return jnp.where(flip, pair[0], pair[1]), jnp.where(flip, pair[1], pair[0])


def share_kernel(nzb, where_ref, act_ref, mine_ref):
    near, _, width = mine_ref.shape
    part, ny = width // 2, near // nzb
    h = where_ref[1]
    for k in range(near):
        zb, y = k // ny, k % ny
        for side, far in enumerate((1 - h, h)):
            start = ((y * 2 + far) * nzb + zb) * part
            block = act_ref[:, pl.ds(pl.multiple_of(start, part), part)]
            mine_ref[k, :, side * part : (side + 1) * part] = block


def share_of(where, activations, nzb, ny, share, part):
    shape = (nzb * ny, share, 2 * part)
    return pl.pallas_call(
        functools.partial(share_kernel, nzb),
        out_shape=jax.ShapeDtypeStruct(shape, activations.dtype),
        grid_spec=pltpu.PrefetchScalarGridSpec(
            num_scalar_prefetch=1,
            grid=(1,),
            in_specs=[pl.BlockSpec((share, activations.shape[1]), lambda i, where: (where[0], 0))],
            out_specs=pl.BlockSpec(shape, lambda i, where: (0, 0, 0)),
        ),
        name="share",
    )(where, activations)


def copies_kernel(seq_len, where_ref, lengths_ref, own_ref, other_ref, copies_ref):
    half, cols = own_ref.shape
    index = where_ref[2] * half + lax.broadcasted_iota(jnp.int32, (half, cols), 0)
    live = None
    for k in range(lengths_ref.shape[0]):
        inside = (index >= k * seq_len) & (index < k * seq_len + lengths_ref[k])
        live = inside if live is None else live | inside
    for side, ref in enumerate((own_ref, other_ref)):
        block = ref[...].astype(F32)
        block = jnp.where(live, block, jnp.zeros_like(block)).astype(copies_ref.dtype)
        for k in range(copies_ref.shape[0]):
            copies_ref[k, :, side * cols : (side + 1) * cols] = block


def copies_of(where, lengths, value_grads, other, count):
    half, cols = other.shape
    shape = (count, half, 2 * cols)
    return pl.pallas_call(
        functools.partial(copies_kernel, value_grads.shape[0] // lengths.shape[0]),
        out_shape=jax.ShapeDtypeStruct(shape, value_grads.dtype),
        grid_spec=pltpu.PrefetchScalarGridSpec(
            num_scalar_prefetch=2,
            grid=(1,),
            in_specs=[
                pl.BlockSpec((half, cols), lambda i, where, lengths: (where[2], 0)),
                pl.BlockSpec((half, cols), lambda i, where, lengths: (0, 0)),
            ],
            out_specs=pl.BlockSpec(shape, lambda i, where, lengths: (0, 0, 0)),
        ),
        name="copies",
    )(where, lengths, value_grads, other)


def outer_kernel(half, x_ref, *refs):
    *pieces, grads_ref, out_ref = refs
    ny, nzb, tok, _ = grads_ref.shape
    share = tok // len(pieces)
    cols = out_ref.shape[1]
    total = None
    for k, piece in enumerate(pieces):
        start = pl.multiple_of((x_ref[0] ^ k) * share, share)
        grads = [
            grads_ref[y, zb, pl.ds(start, share), half * cols : (half + 1) * cols]
            for zb in range(nzb)
            for y in range(ny)
        ]
        term = lax.dot_general(
            piece[...],
            jnp.concatenate(grads, axis=0),
            (((0,), (0,)), ((), ())),
            preferred_element_type=F32,
        )
        total = term if total is None else total + term
    out_ref[...] = total.astype(out_ref.dtype)


def outer(x, pieces, grads, half, dtype):
    rows, cols = pieces[0].shape[1], grads.shape[3] // 2
    vmem = pl.BlockSpec(memory_space=pltpu.VMEM)
    depth = sum(piece.shape[0] for piece in pieces)
    return pl.pallas_call(
        functools.partial(outer_kernel, half),
        out_shape=jax.ShapeDtypeStruct((rows, cols), dtype),
        in_specs=[pl.BlockSpec(memory_space=pltpu.SMEM)] + [vmem] * (len(pieces) + 1),
        out_specs=vmem,
        cost_estimate=pl.CostEstimate(
            flops=2 * depth * rows * cols,
            bytes_accessed=2 * depth * (rows + cols),
            transcendentals=0,
        ),
        compiler_params=pltpu.CompilerParams(vmem_limit_bytes=SMALL),
    )(x.reshape(1), *pieces, grads)


def step(activations, value_grads, lengths, master, moment_one, moment_two):
    tok, _ = activations.shape
    rows, cols = master.shape
    nzb, ny, nx = lax.axis_size("zb"), lax.axis_size("y"), lax.axis_size("x")
    near = nzb * ny
    half = tok // 2
    share = half // nx
    part = rows // nzb
    h, c, zb = lax.axis_index("h"), lax.axis_index("c"), lax.axis_index("zb")
    x = lax.axis_index("x")

    send = lax.dynamic_slice_in_dim(value_grads, (1 - c) * half, half, 0)
    vg_other = swapped(send, "c")

    weight = lax.dynamic_slice_in_dim(master, zb * part, part, 0).astype(BF16)
    weight_far = across(weight)

    where = jnp.stack([c * nx + x, h, c]).astype(jnp.int32)
    mine = share_of(where, activations, nzb, ny, share, part)
    act_share = exchanged(mine, NEAR)
    copies = copies_of(where, lengths, value_grads, vg_other, nzb)
    copies, act_share = lax.optimization_barrier((copies, act_share))
    vg_near = exchanged(copies, "zb").reshape(nzb * half, 2 * cols)
    grads = gathered(vg_near, "y").reshape(ny, nzb, half, 2 * cols)
    act_share = act_share.reshape(near * share, 2 * part)
    pieces = [act_share]
    for k in range(1, nx):
        pieces.append(swapped(act_share, "x", k))

    partial = outer(x, pieces, grads, 1, BF16)
    partial = swapped(partial, "c")
    partial = outer(x, pieces, grads, 0, F32) + partial.astype(F32)
    received = across(partial[:part].astype(BF16))
    total = (partial[part:] + received.astype(F32)).astype(BF16)
    for bit in (1, 2):
        if bit < lax.axis_size("za"):
            received = swapped(total, "za", bit)
            total = (total.astype(F32) + received.astype(F32)).astype(BF16)
    grad = gathered(total, "zb").reshape(rows, cols).astype(F32)
    count = float(tok * lax.axis_size(TOKENS))
    new_master, new_one, new_two = adamw(grad / count, master, moment_one, moment_two)

    both = jnp.concatenate(own_first((weight, weight_far), h), axis=0)
    both_other = swapped(both, "c")
    both = jnp.concatenate([both, both_other], axis=1)
    tokens = grads.reshape(near * half, 2 * cols)

    def product(w):
        out = lax.dot_general(tokens, w, (((1,), (1,)), ((), ())), preferred_element_type=F32)
        return out.astype(BF16).reshape(ny, nzb, half, part)

    product = jnp.stack([product(both[:part]), product(both[part:])], axis=1)
    arrived = exchanged(product.reshape(ny * 2, nzb * half, part), COLS)
    block = arrived.reshape(nx, 2, nzb, half, part).astype(F32).sum(axis=0).astype(BF16)
    block = block.transpose(1, 0, 2, 3).reshape(nzb, tok, part)
    block = exchanged(block, "zb")
    block = block.transpose(1, 0, 2).reshape(tok, rows)
    turn = [(y * nx + x, x * nx + y) for y in range(ny) for x in range(nx)]
    input_grads = lax.ppermute(block, ("y", "x"), turn)
    return (input_grads, new_master, new_one, new_two)


def solution(mesh):
    replica, fsdp, tensor = (mesh.shape[a] for a in ("replica", "fsdp", "tensor"))
    near = 4 if replica == 16 else 2
    split = Mesh(
        mesh.devices.reshape(replica // near, near, fsdp // 2, 2, tensor // 2, 2), AXES
    )
    in_specs = (
        P(TOKENS, None),
        P(TOKENS, COLS),
        P(TOKENS),
        P(ROWS, COLS),
        P(ROWS, COLS),
        P(ROWS, COLS),
    )
    out_specs = (P(TOKENS, COLS), P(ROWS, COLS), P(ROWS, COLS), P(ROWS, COLS))
    return jax.shard_map(
        step, mesh=split, in_specs=in_specs, out_specs=out_specs, check_vma=False
    )
```
